512 devices in a mesh: traj: 16 (over z, core), space: 32 (over y, x).
Axes of the slice: x: 4, y: 8, z: 8, core: 2. Of those that a mesh axis runs over, the one named last changes fastest.
Arguments:
- base_state: float32 [256, 1024], P('space'), may hold values from -3 to 3
- perturbations: float32 [16, 16, 256, 1024], P('traj', None, 'space'), may hold values from -2 to 2
- sketch: float32 [256, 16], replicated, may hold values from -0.375 to 0.375
Outputs:
- basis: float32 [16, 256, 1024], P(None, 'space')
The draws below stay inside these ranges and needn't reach their ends.
All inputs are finite; a program needn't handle non-finite values.
Results may differ from the reference program's by a relative error of at most 0.00027.
Values sent between devices are 32-bit elements; how exact they have to be, the bound alone decides.
A program may use at most 64 MiB of HBM per device.

```python
import jax
import jax.numpy as jnp
from jax import lax

NX = 1024
PERT = 16
RANK = 16
STEPS = 4
GROUPS = 16
NY = 256
COLS = 256
CELLS = 262144


def levels(own_key, shape, pieces, smallest, top_value):
    def one(dim, blocks):
        steps = jax.random.uniform(jax.random.fold_in(jax.random.fold_in(own_key, 6), dim), (blocks,), jnp.float32, smallest / len(pieces), top_value / len(pieces))
        return jnp.repeat(jnp.exp(steps), shape[dim] // blocks).reshape((-1,) + (1,) * (len(shape) - dim - 1))

    factor_of = one(*pieces[0])
    for cut in pieces[1:]:
        factor_of = factor_of * one(*cut)
    return factor_of


def noise(stream_key, extent, width, bound, split=(), dtype=jnp.bfloat16):
    entries = jax.random.normal(stream_key, extent, jnp.float32) * width
    if len(split) > 0:
        entries = levels(stream_key, extent, split, -0.22, 0.18) * entries
    return jnp.clip(entries, min=-bound, max=bound).astype(dtype)


def setup_inputs(seed: int = 0) -> dict:
    arg_keys = jax.random.split(jax.random.key(seed), 4)
    return {
        "base_state": noise(arg_keys[0], (NY, NX), 0.5, 3.0, ((0, 32),), jnp.float32),
        "perturbations": noise(arg_keys[1], (GROUPS, PERT, NY, NX), 0.3, 2.0, ((0, 16), (2, 32)), jnp.float32),
        "sketch": noise(arg_keys[2], (COLS, RANK), COLS ** -0.5, 0.375, (), jnp.float32),
    }


diffusion = 0.4
advection = 0.5
time_step = 0.5

def tendency(field):
    center = field[:, 1:-1, :]
    above_row = field[:, 2:, :]
    below_row = field[:, :-2, :]
    east_side = jnp.roll(center, -1, axis=2)
    west_side = jnp.roll(center, 1, axis=2)
    lap_term = above_row + below_row + east_side + west_side - 4.0 * center
    slope = east_side - west_side + (above_row - below_row)
    return diffusion * lap_term - 0.5 * advection * center * slope

def pad_rows(field):
    return jnp.pad(field, ((0, 0), (1, 1), (0, 0)))

def advance(fields):
    for repeat in range(STEPS):
        section_one = fields + time_step * tendency(pad_rows(fields))
        section_two = 0.75 * fields + 0.25 * (section_one + time_step * tendency(pad_rows(section_one)))
        fields = fields * (1.0 / 3.0) + 2.0 / 3.0 * (section_two + time_step * tendency(pad_rows(section_two)))
    return fields

def reference(base_state, perturbations, sketch):
    final_base = advance(base_state[None])

    def one_group(group_pert):
        return advance(base_state[None] + group_pert) - final_base
    snapshots = lax.map(one_group, perturbations)
    matrix = snapshots.reshape(COLS, CELLS)
    highest = lax.Precision.HIGHEST
    gram = jnp.dot(matrix.astype(jnp.float32), matrix.T.astype(jnp.float32), precision=highest, preferred_element_type=jnp.float32) / CELLS
    weights = jnp.dot(gram.astype(jnp.float32), sketch.astype(jnp.float32), precision=highest, preferred_element_type=jnp.float32)
    projected = jnp.dot(weights.T.astype(jnp.float32), matrix.astype(jnp.float32), precision=highest, preferred_element_type=jnp.float32)
    small_gram = jnp.dot(projected.astype(jnp.float32), projected.T.astype(jnp.float32), precision=highest, preferred_element_type=jnp.float32) / CELLS
    lower = jnp.linalg.cholesky(small_gram)
    basis = lax.linalg.triangular_solve(lower, projected, left_side=True, lower=True)
    return basis.reshape(RANK, NY, NX)
```

```python
import functools

import jax
import jax.numpy as jnp
from jax import lax
from jax.experimental import pallas as pl
from jax.experimental.pallas import tpu as pltpu
from jax.sharding import Mesh
from jax.sharding import PartitionSpec as P

STEPS = 4
CORES = 2
ALONG_X = 4
HALO_TILES = 2
MESH = pl.DeviceIdType.MESH
F32 = jnp.float32


def shifted(c):
    lane = lax.broadcasted_iota(jnp.int32, c.shape, c.ndim - 1)
    a, s = c.ndim - 1, c.ndim - 2
    e = pltpu.roll(c, 127, a)
    e = jnp.where(lane == 127, pltpu.roll(e, 7, s), e)
    w = pltpu.roll(c, 1, a)
    w = jnp.where(lane == 0, pltpu.roll(w, 1, s), w)
    return e, w


def parts_of(lo, hi, first, last):
    cuts = [lo]
    while cuts[-1] < hi:
        at = cuts[-1]
        if at < first:
            at = min(first, hi)
        elif at < last:
            at = min(at + 8, last)
        else:
            at = hi
        cuts.append(at)
    return list(zip(cuts[:-1], cuts[1:]))


def stage(src, field, dst, lo, hi, first, last, low, high, mix):
    keep, take = mix
    for r0, r1 in parts_of(lo, hi, first, last):
        c = src[r0:r1]
        e, w = shifted(c)
        p = e + src[r0 + 1 : r1 + 1]
        m = w + src[r0 - 1 : r1 - 1]
        out = (0.2 * take) * ((p + m) + c) - ((0.125 * take) * c) * (p - m)
        if keep:
            out = keep * field[r0:r1] + out
        if r1 <= first:
            out = out * low
        elif r0 >= last:
            out = out * high
        dst[r0:r1] = out


def advance(v, w1, w2, first, last, low, high):
    lo, hi = first - 3 * STEPS, last + 3 * STEPS
    for _ in range(STEPS):
        args = (first, last, low, high)
        stage(v, v, w1, lo + 1, hi - 1, *args, (0.0, 1.0))
        stage(w1, v, w2, lo + 2, hi - 2, *args, (0.75, 0.25))
        stage(w2, v, v, lo + 3, hi - 3, *args, (1.0 / 3.0, 2.0 / 3.0))
        lo, hi = lo + 3, hi - 3


def peers_of(dims):
    X, Y, Z, C = dims
    x, y, z, c = (lax.axis_index(n) for n in "xyzc")

    def column(n):
        return {"c": lax.rem(c + lax.rem(n, C), C), "z": lax.rem(z + n // C, Z)}

    def plane(n):
        return {"x": lax.rem(x + lax.rem(n, X), X), "y": lax.rem(y + n // X, Y)}

    return column, plane


def each(count, do):
    def step(n, carry):
        do(n)
        return carry

    lax.fori_loop(1, count, step, 0)


def snapshots_body(dims, base_ref, pert_ref, got, raw, basein, bv, v, w1, w2, fb, send, xs_send, xs_recv, own_sem, y_send, y_recv, a_send, a_recv):
    X, Y, Z, C = dims
    TL = raw.shape[0]
    KB = TL // 2
    NS = X * Z * C
    first, last = 8 * HALO_TILES, 8 * (HALO_TILES + X)
    x, y, z, c = (lax.axis_index(n) for n in "xyzc")
    me = (z * C + c) * X + x
    below, above = y > 0, y < Y - 1
    low = jnp.where(below, 1.0, 0.0).astype(F32)
    high = jnp.where(above, 1.0, 0.0).astype(F32)

    def target(n):
        return {
            "x": lax.rem(x + lax.rem(n // C, X), X),
            "c": lax.rem(c + lax.rem(n, C), C),
            "z": lax.rem(z + n // (C * X), Z),
        }

    barrier = pltpu.get_barrier_semaphore()

    def greet(n, carry):
        pl.semaphore_signal(barrier, inc=1, device_id=target(n), device_id_type=MESH)
        return carry

    lax.fori_loop(1, NS, greet, 0)
    column, plane = peers_of(dims)

    def greet_plane(n, carry):
        pl.semaphore_signal(barrier, inc=1, device_id=plane(n), device_id_type=MESH)
        return carry

    lax.fori_loop(X, X * Y, greet_plane, 0)
    pl.semaphore_wait(barrier, NS - 1 + X * Y - X)

    def x_copy(t, d):
        to = lax.rem(x + d, X)
        source = base_ref if t is None else pert_ref.at[to * TL + t]
        dest = basein.at[HALO_TILES + x] if t is None else raw.at[t, HALO_TILES + x]
        slot = TL if t is None else t
        return pltpu.make_async_remote_copy(
            source, dest, xs_send.at[slot, d], xs_recv.at[slot, d], device_id={"x": to}, device_id_type=MESH
        )

    def own_copy(t):
        source = base_ref if t is None else pert_ref.at[x * TL + t]
        dest = basein.at[HALO_TILES + x] if t is None else raw.at[t, HALO_TILES + x]
        return pltpu.make_async_copy(source, dest, own_sem.at[TL if t is None else t])

    order = [d for d in (1, X - 1, 2) if d < X]
    order = list(dict.fromkeys(order))
    for t in [None, *range(TL)]:
        own_copy(t).start()
        for d in order:
            x_copy(t, d).start()

    def up(t):
        buf = basein if t is None else raw.at[t]
        slot = TL if t is None else t
        return pltpu.make_async_remote_copy(
            buf.at[pl.ds(X, 2)], buf.at[pl.ds(0, 2)], y_send.at[slot, 0], y_recv.at[slot, 0],
            device_id={"y": y + 1}, device_id_type=MESH,
        )

    def down(t):
        buf = basein if t is None else raw.at[t]
        slot = TL if t is None else t
        return pltpu.make_async_remote_copy(
            buf.at[pl.ds(2, 2)], buf.at[pl.ds(X + 2, 2)], y_send.at[slot, 1], y_recv.at[slot, 1],
            device_id={"y": y - 1}, device_id_type=MESH,
        )

    def arrive_x(t):
        own_copy(t).wait()
        for d in order:
            x_copy(t, d).wait_recv()

    def pass_on(t):
        @pl.when(above)
        def _():
            up(t).start()

        @pl.when(below)
        def _():
            down(t).start()

    def arrive_y(t):
        buf = basein if t is None else raw.at[t]

        @pl.when(below)
        def _():
            up(t).wait_recv()

        @pl.when(above)
        def _():
            down(t).wait_recv()

        @pl.when(jnp.logical_not(below))
        def _():
            buf[0:2] = jnp.zeros((2, 64, 128), F32)

        @pl.when(jnp.logical_not(above))
        def _():
            buf[X + 2 : X + 4] = jnp.zeros((2, 64, 128), F32)

    def rows_of(buf, row):
        return buf[row // 8, pl.ds(row % 8, 8, stride=8), :]

    for t in [None, 0, 1]:
        arrive_x(t)
        pass_on(t)
    arrive_y(None)
    for row in range(first - 12, last + 12):
        val = rows_of(basein, row)
        bv[row] = val
        v[row] = val
    advance(v, w1, w2, first, last, low, high)
    for i in range(X):
        fb[8 * i : 8 * i + 8] = v[first + 8 * i : first + 8 * i + 8]

    def out_copy(b, n):
        to = target(n)
        return pltpu.make_async_remote_copy(
            send.at[b, to["x"], to["z"], to["c"]], got.at[b, pl.ds(pl.multiple_of(8 * me, 8), 8)], a_send.at[b], a_recv.at[b],
            device_id=to, device_id_type=MESH,
        )

    def mine(b):
        return pltpu.make_async_copy(send.at[b, x, z, c], got.at[b, pl.ds(pl.multiple_of(8 * me, 8), 8)], a_recv.at[b])

    def pair(b, carry):
        for f in range(2):
            t = 2 * b + f

            @pl.when(t + 2 < TL)
            def _():
                arrive_x(t + 2)
                pass_on(t + 2)

            arrive_y(t)
            for row in range(first - 12, last + 12):
                v[row] = bv[row] + rows_of(raw.at[t], row)
            advance(v, w1, w2, first, last, low, high)
            half = lax.broadcasted_iota(jnp.int32, (8, 8, 128), 1) < 4
            for i in range(X):
                snap = v[first + 8 * i : first + 8 * i + 8] - fb[8 * i : 8 * i + 8]
                turned = pltpu.roll(snap, 4, 1)
                if f == 0:
                    send[b, i, :, 0] = snap
                    send[b, i, :, 1] = turned
                else:
                    send[b, i, :, 0] = jnp.where(half, send[b, i, :, 0], turned)
                    send[b, i, :, 1] = jnp.where(half, send[b, i, :, 1], snap)

        def give(n, carry):
            out_copy(b, n).start()
            return carry

        mine(b).start()
        lax.fori_loop(1, NS, give, 0)
        return carry

    lax.fori_loop(0, KB, pair, 0)


    def finish():
        for t in [None, *range(TL)]:
            for d in order:
                x_copy(t, d).wait_send()

            @pl.when(above)
            def _():
                up(t).wait_send()

            @pl.when(below)
            def _():
                down(t).wait_send()

        for b in range(KB):
            others = got.at[b, pl.ds(0, 8 * NS - 8)]
            pltpu.make_async_copy(others, others, a_send.at[b]).wait()

    return finish


def inverse_factor(gram):
    row = lax.broadcasted_iota(jnp.int32, (16, 128), 0)
    lane = lax.broadcasted_iota(jnp.int32, (16, 128), 1)
    a = jnp.where(lane < 16, gram, jnp.where(lane == row + 16, 1.0, 0.0))
    for k in range(16):
        scale = 1.0 / jnp.sqrt(a[k : k + 1, k : k + 1])
        pivot = a[k : k + 1, :] * scale
        factor = a[:, k : k + 1] * scale
        a = jnp.where(row > k, a - factor * pivot, jnp.where(row == k, pivot, a))
    return a


def reduce_body(dims, omega_ref, out_ref, got, a_recv, S, wsend, wrecv, own, own_row, plane_recv, w_all, psend, pall, small, small_plane, small_column, sems):
    X, Y, Z, C = dims
    KB = got.shape[0]
    TL = 2 * KB
    NZC, NXY, NS = Z * C, X * Y, X * Z * C
    cells = Y * X * 8 * 1024
    x, y, z, c = (lax.axis_index(n) for n in "xyzc")
    mine, here = z * C + c, y * X + x
    column, plane = peers_of(dims)

    def dot(a, b, dims):
        return lax.dot_general(a, b, (dims, ((), ())), precision=lax.Precision.HIGHEST, preferred_element_type=F32)

    for b in range(KB):
        everything = got.at[b]
        pltpu.make_async_copy(everything, everything, a_recv.at[b]).wait()
        for f in range(2):
            for q in range(4):
                S[q, pl.ds(2 * b + f, NS, stride=TL), :] = got[b, pl.ds(4 * f + q, NS, stride=8), :]
    mat = jnp.concatenate([S[q] for q in range(4)], axis=1)
    sketched = dot(omega_ref[...], mat, ((1,), (0,)))
    part = dot(sketched, mat, ((1,), (1,))) * (1.0 / cells)
    for h in range(2):
        wsend[h] = part[:, 128 * h : 128 * h + 128]

    def remote(src, dst, k, n, to):
        return pltpu.make_async_remote_copy(
            src, dst, sems.at[0, k, n], sems.at[1, k, n], device_id=to, device_id_type=MESH
        )

    def scatter(n):
        to = column(n)
        row = to["z"] * C + to["c"]
        return remote(wsend.at[:, pl.ds(row, 1), :], wrecv.at[:, pl.ds(mine, 1), :], 0, n, to)

    def spread(n):
        return remote(own, plane_recv.at[here], 1, n, plane(n))

    def gather(n):
        return remote(own_row.at[:, pl.ds(0, 1), :], w_all.at[:, pl.ds(mine, 1), :], 2, n, column(n))

    def projected(n):
        return remote(psend, pall.at[pl.ds(4 * c, 4), :, z, :], 3, n, column(n))

    def small_spread(n):
        return remote(small.at[0], small_plane.at[here], 4, n, plane(n))

    def small_gather(n):
        return remote(small.at[1], small_column.at[mine], 5, n, column(n))

    each(NZC, lambda n: scatter(n).start())
    wrecv[:, pl.ds(mine, 1), :] = wsend[:, pl.ds(mine, 1), :]
    each(NZC, lambda n: scatter(n).wait_recv())
    value = jnp.sum(wrecv[...], axis=1)
    own[...] = value
    each(NXY, lambda n: spread(n).start())
    plane_recv[here] = value
    each(NXY, lambda n: spread(n).wait_recv())
    value = jnp.sum(plane_recv[...], axis=0)
    for h in range(2):
        own_row[h, 0:1, :] = value[h : h + 1]
    each(NZC, lambda n: gather(n).start())
    for h in range(2):
        w_all[h, pl.ds(mine, 1), :] = value[h : h + 1]
    each(NZC, lambda n: gather(n).wait_recv())
    weights = jnp.concatenate([w_all[0], w_all[1]], axis=1)
    proj = dot(weights, mat, ((1,), (0,)))
    for q in range(4):
        psend[q] = proj[:, 128 * q : 128 * q + 128]
    each(NZC, lambda n: projected(n).start())
    own_p = pltpu.make_async_copy(psend, pall.at[pl.ds(4 * c, 4), :, z, :], sems.at[0, 3, 0])
    own_p.start()

    row = lax.broadcasted_iota(jnp.int32, (16, 128), 0)
    lane = lax.broadcasted_iota(jnp.int32, (16, 128), 1)
    diagonal = lane // 16 == lax.rem(row, 8)
    wide = dot(proj, jnp.concatenate([proj] * 8, axis=0), ((1,), (1,))) * (1.0 / cells)
    wide = jnp.where(diagonal, wide, 0.0)
    value = jnp.concatenate([jnp.sum(wide[8 * h : 8 * h + 8], axis=0, keepdims=True) for h in range(2)], axis=0)
    small[0] = value
    each(NXY, lambda n: small_spread(n).start())
    small_plane[here] = value
    each(NXY, lambda n: small_spread(n).wait_recv())
    value = jnp.sum(small_plane[...], axis=0)
    small[1] = value
    each(NZC, lambda n: small_gather(n).start())
    small_column[mine] = value
    each(NZC, lambda n: small_gather(n).wait_recv())
    value = jnp.sum(small_column[...], axis=0)
    gram = jnp.concatenate([jnp.broadcast_to(value[h : h + 1], (8, 128)) for h in range(2)], axis=0)
    gram = jnp.where(diagonal, gram, 0.0)
    for shift in (64, 32, 16):
        gram = gram + pltpu.roll(gram, shift, 1)
    inverse = inverse_factor(gram)

    own_p.wait()
    each(NZC, lambda n: projected(n).wait_recv())
    for i in range(16):
        total = inverse[i : i + 1, 16:17] * pall[:, 0]
        for m in range(1, i + 1):
            total = total + inverse[i : i + 1, 16 + m : 17 + m] * pall[:, m]
        out_ref[i] = total

    each(NZC, lambda n: scatter(n).wait_send())
    each(NXY, lambda n: spread(n).wait_send())
    each(NZC, lambda n: gather(n).wait_send())
    each(NZC, lambda n: projected(n).wait_send())
    each(NXY, lambda n: small_spread(n).wait_send())
    each(NZC, lambda n: small_gather(n).wait_send())


def whole_body(dims, base_ref, pert_ref, omega_ref, out_ref, *scratch):
    got, one, two = scratch[0], scratch[1:16], scratch[16:]
    finish = snapshots_body(dims, base_ref, pert_ref, got, *one)
    reduce_body(dims, omega_ref, out_ref, got, one[-1], *two)
    finish()


def basis_of(base, pert, omega, dims):
    X, Y, Z, C = dims
    TL = pert.shape[0] // X
    KB, NS, NZC, NXY = TL // 2, X * Z * C, Z * C, X * Y
    rows = 8 * (X + 2 * HALO_TILES)
    sem = pltpu.SemaphoreType.DMA
    anywhere = pl.BlockSpec(memory_space=pl.ANY)
    inside = pl.BlockSpec(memory_space=pltpu.VMEM)
    vmem = lambda *shape: pltpu.VMEM(shape, F32)
    return pl.pallas_call(
        functools.partial(whole_body, dims),
        out_shape=jax.ShapeDtypeStruct((16, 8, 8, 128), F32),
        in_specs=[anywhere, anywhere, inside],
        out_specs=inside,
        scratch_shapes=[
            vmem(KB, NS * 8, 128),
            vmem(TL, rows // 8, 64, 128),
            vmem(rows // 8, 64, 128),
            vmem(rows, 8, 128),
            vmem(rows, 8, 128),
            vmem(rows, 8, 128),
            vmem(rows, 8, 128),
            vmem(8 * X, 8, 128),
            vmem(KB, X, Z, C, 8, 128),
            sem((TL + 1, X)),
            sem((TL + 1, X)),
            sem((TL + 1,)),
            sem((TL + 1, 2)),
            sem((TL + 1, 2)),
            sem((KB,)),
            sem((KB,)),
            vmem(4, NS * TL, 128),
            vmem(2, 16, 128),
            vmem(2, 16, 128),
            vmem(2, 128),
            vmem(2, 8, 128),
            vmem(NXY, 2, 128),
            vmem(2, 16, 128),
            vmem(4, 16, 128),
            vmem(8, 16, 8, 128),
            vmem(2, 2, 128),
            vmem(NXY, 2, 128),
            vmem(NZC, 2, 128),
            sem((2, 6, max(NXY, NZC))),
        ],
        compiler_params=pltpu.CompilerParams(collective_id=0, has_side_effects=True),
    )(base, pert, omega)


def tiles_first(a):
    lead = a.shape[:-2]
    a = a.reshape(*lead, 8, 8, 128)
    n = len(lead)
    return a.transpose(*range(n), n + 1, n, n + 2).reshape(*lead, 64, 128)


def body(dims, base_state, perturbations, sketch):
    out = basis_of(tiles_first(base_state), tiles_first(perturbations[0]), sketch.T, dims)
    return out.transpose(0, 2, 1, 3).reshape(16, 8, 1024)


def solution(mesh, along_x=ALONG_X):
    traj, space = mesh.shape["traj"], mesh.shape["space"]
    dims = (along_x, space // along_x, traj // CORES, CORES)
    X, Y, Z, C = dims
    torus = Mesh(mesh.devices.reshape(Z, C, Y, X), ("z", "c", "y", "x"))
    return jax.shard_map(
        functools.partial(body, dims),
        mesh=torus,
        in_specs=(P(("y", "x"), None), P(("z", "c"), None, ("y", "x"), None), P()),
        out_specs=P(None, ("y", "x"), None),
        check_vma=False,
    )
```

```python
import functools

import jax
import jax.numpy as jnp
from jax import lax
from jax.experimental import pallas as pl
from jax.experimental.pallas import tpu as pltpu
from jax.sharding import Mesh
from jax.sharding import PartitionSpec as P

STEPS = 4
CORES = 2
ALONG_X = 4
HALO_TILES = 2
MESH = pl.DeviceIdType.MESH
F32 = jnp.float32


def shifted(c):
    lane = lax.broadcasted_iota(jnp.int32, c.shape, c.ndim - 1)
    a, s = c.ndim - 1, c.ndim - 2
    e = pltpu.roll(c, 127, a)
    e = jnp.where(lane == 127, pltpu.roll(e, 7, s), e)
    w = pltpu.roll(c, 1, a)
    w = jnp.where(lane == 0, pltpu.roll(w, 1, s), w)
    return e, w


def parts_of(lo, hi, first, last):
    cuts = [lo]
    while cuts[-1] < hi:
        at = cuts[-1]
        if at < first:
            at = min(first, hi)
        elif at < last:
            at = min(at + 8, last)
        else:
            at = hi
        cuts.append(at)
    return list(zip(cuts[:-1], cuts[1:]))


def stage(src, field, dst, lo, hi, first, last, low, high, mix):
    keep, take = mix
    for r0, r1 in parts_of(lo, hi, first, last):
        c = src[r0:r1]
        e, w = shifted(c)
        p = e + src[r0 + 1 : r1 + 1]
        m = w + src[r0 - 1 : r1 - 1]
        out = (0.2 * take) * ((p + m) + c) - ((0.125 * take) * c) * (p - m)
        if keep:
            out = keep * field[r0:r1] + out
        if r1 <= first:
            out = out * low
        elif r0 >= last:
            out = out * high
        dst[r0:r1] = out


def advance(v, w1, w2, first, last, low, high):
    lo, hi = first - 3 * STEPS, last + 3 * STEPS
    for _ in range(STEPS):
        args = (first, last, low, high)
        stage(v, v, w1, lo + 1, hi - 1, *args, (0.0, 1.0))
        stage(w1, v, w2, lo + 2, hi - 2, *args, (0.75, 0.25))
        stage(w2, v, v, lo + 3, hi - 3, *args, (1.0 / 3.0, 2.0 / 3.0))
        lo, hi = lo + 3, hi - 3


def wrapped(at, size):
    return [at] + [jnp.where(at + d < size, at + d, at + d - size) for d in range(1, size)]


def far_first(size):
    return sorted(range(size), key=lambda d: (-min(d, size - d), d))


def settle(like, sem):
    pltpu.make_async_copy(like, like, sem).wait()


class Places:
    def __init__(self, dims):
        X, Y, Z, C = self.dims = dims
        self.x, self.y, self.z, self.c = (lax.axis_index(n) for n in "xyzc")
        self.xs, self.ys = wrapped(self.x, X), wrapped(self.y, Y)
        self.zs, self.cs = wrapped(self.z, Z), wrapped(self.c, C)
        self.column = [(dz, dc) for dz in far_first(Z) for dc in range(C) if dz or dc]
        self.plane = sorted(
            ((dy, dx) for dy in range(Y) for dx in range(X) if dy or dx),
            key=lambda d: -min(d[0], Y - d[0]) - min(d[1], X - d[1]),
        )
        self.all = sorted(
            ((dz, dc, dx) for dz in range(Z) for dc in range(C) for dx in range(X) if dz or dc or dx),
            key=lambda d: -min(d[0], Z - d[0]) - min(d[2], X - d[2]),
        )


def snapshots_body(at, base_ref, pert_ref, got, pertv, basev, raw, v, w1, w2, send, in_sem, hello, xs_send, xs_recv, y_send, y_recv, a_send, a_recv):
    X, Y, Z, C = at.dims
    TL = raw.shape[0] - 1
    NS = X * Z * C
    first, last = 8 * HALO_TILES, 8 * (HALO_TILES + X)
    x, y, z, c = at.x, at.y, at.z, at.c
    me = (z * C + c) * X + x
    below, above = y > 0, y < Y - 1
    low = jnp.where(below, 1.0, 0.0).astype(F32)
    high = jnp.where(above, 1.0, 0.0).astype(F32)
    order = far_first(X)[:-1]
    rounds = max(Z, Y) // 2

    def signal(sem, to):
        pl.semaphore_signal(sem, inc=1, device_id=to, device_id_type=MESH)

    barrier = pltpu.get_barrier_semaphore()
    for dx in range(X):
        for dc in range(C):
            if dx or dc:
                signal(barrier, {"x": at.xs[dx], "c": at.cs[dc]})
    around = [{"z": at.zs[1]}, {"z": at.zs[Z - 1]}, {"y": at.ys[1]}, {"y": at.ys[Y - 1]}]
    for to in around:
        signal(barrier, to)

    base_in = pltpu.make_async_copy(base_ref, basev, in_sem.at[0])
    pert_in = pltpu.make_async_copy(pert_ref, pertv, in_sem.at[1])
    base_in.start()
    pert_in.start()
    base_in.wait()
    pert_in.wait()
    for k in range(X * TL):
        pertv[k] = pertv[k] + basev[...]
    pl.semaphore_wait(barrier, X * C - 1 + 4)

    def greet(k):
        for to in around:
            signal(hello.at[k], to)

    def greeted(k):
        pl.semaphore_wait(hello.at[k], 4)

    def x_copy(t, d):
        to = at.xs[d]
        source = basev if isinstance(t, int) and t == TL else pertv.at[to * TL + t]
        return pltpu.make_async_remote_copy(
            source, raw.at[t, HALO_TILES + x], xs_send, xs_recv.at[t],
            device_id={"x": to}, device_id_type=MESH,
        )

    for t in range(TL + 1):
        for d in order:
            x_copy(t, d).start()
    greet(0)
    for t in range(TL):
        raw[t, HALO_TILES + x] = pertv[x * TL + t]
    raw[TL, HALO_TILES + x] = basev[...]

    def up(t):
        buf = raw.at[t]
        return pltpu.make_async_remote_copy(
            buf.at[pl.ds(X, 2)], buf.at[pl.ds(0, 2)], y_send.at[0], y_recv.at[t, 0],
            device_id={"y": y + 1}, device_id_type=MESH,
        )

    def down(t):
        buf = raw.at[t]
        return pltpu.make_async_remote_copy(
            buf.at[pl.ds(2, 2)], buf.at[pl.ds(X + 2, 2)], y_send.at[1], y_recv.at[t, 1],
            device_id={"y": y - 1}, device_id_type=MESH,
        )

    def arrive_x(t):
        settle(raw.at[t, pl.ds(0, X - 1)], xs_recv.at[t])

    def pass_on(t):
        @pl.when(above)
        def _():
            up(t).start()

        @pl.when(below)
        def _():
            down(t).start()

    def arrive_y(t):
        buf = raw.at[t]

        @pl.when(below)
        def _():
            up(t).wait_recv()

        @pl.when(above)
        def _():
            down(t).wait_recv()

        @pl.when(jnp.logical_not(below))
        def _():
            buf[0:2] = jnp.zeros((2, 64, 128), F32)

        @pl.when(jnp.logical_not(above))
        def _():
            buf[X + 2 : X + 4] = jnp.zeros((2, 64, 128), F32)

    def rows_of(buf, row):
        return buf[row // 8, pl.ds(row % 8, 8, stride=8), :]

    for k in range(rounds - 2):
        greeted(k)
        greet(k + 1)
    arrive_x(0)
    pass_on(0)
    greeted(rounds - 2)
    greet(rounds - 1)
    arrive_x(1)
    pass_on(1)

    def spot(t):
        return got.at[t, pl.ds(pl.multiple_of(4 * me, 4), 4), :]

    def cells(t, xx, zz, cc):
        return send.at[t, xx, zz, pl.ds(pl.multiple_of(4 * cc, 4), 4), :]

    def one(t, carry):
        arrive_y(t)
        for row in range(first - 12, last + 12):
            v[row] = rows_of(raw.at[t], row)
        advance(v, w1, w2, first, last, low, high)

        @pl.when(t == 0)
        def _():
            greeted(rounds - 1)

        @pl.when(t < TL)
        def _():
            for i in range(X):
                send[t, i] = v[first + 8 * i : first + 8 * i + 8]
            pltpu.make_async_copy(cells(t, x, z, c), spot(t), a_recv.at[t]).start()
            for dz, dc, dx in at.all:
                zz, cc, xx = at.zs[dz], at.cs[dc], at.xs[dx]
                pltpu.make_async_remote_copy(
                    cells(t, xx, zz, cc), spot(t), a_send, a_recv.at[t],
                    device_id={"x": xx, "z": zz, "c": cc}, device_id_type=MESH,
                ).start()

        @pl.when(t + 2 < TL + 1)
        def _():
            arrive_x(t + 2)
            pass_on(t + 2)

        return carry

    lax.fori_loop(0, TL + 1, one, 0)

    def finish():
        settle(raw.at[:, pl.ds(0, X - 1)], xs_send)

        @pl.when(above)
        def _():
            settle(raw.at[:, pl.ds(0, 2)], y_send.at[0])

        @pl.when(below)
        def _():
            settle(raw.at[:, pl.ds(0, 2)], y_send.at[1])

        settle(got.at[:, pl.ds(0, 4 * NS - 4)], a_send)

    return finish


def inverse_factor(gram):
    row = lax.broadcasted_iota(jnp.int32, (16, 128), 0)
    lane = lax.broadcasted_iota(jnp.int32, (16, 128), 1)
    a = jnp.where(lane < 16, gram, jnp.where(lane == row + 16, 1.0, 0.0))
    def wide(col):
        return jnp.broadcast_to(col, (16, 128))

    for k in range(0, 14, 2):
        p0, p1 = wide(a[k : k + 1, :]), wide(a[k + 1 : k + 2, :])
        f0, f1 = wide(a[:, k : k + 1]), wide(a[:, k + 1 : k + 2])
        u, v, w = wide(p0[:, k : k + 1]), wide(p0[:, k + 1 : k + 2]), wide(p1[:, k + 1 : k + 2])
        scale = 1.0 / (u * w - v * v)
        change = ((f0 * w - f1 * v) * scale) * p0 + ((f1 * u - f0 * v) * scale) * p1
        a = jnp.where(row > k + 1, a - change, a)
    before = pltpu.roll(a, 1, 0)
    cross = jnp.sum(jnp.where(lane == row - 1, a, 0.0), axis=1, keepdims=True)
    first = jnp.sum(jnp.where(lane == row - 1, before, 0.0), axis=1, keepdims=True)
    odd = lax.rem(row, 2) == 1
    a = jnp.where(odd, a - cross / first * before, a)
    diagonal = jnp.sum(jnp.where(lane == row, a, 0.0), axis=1, keepdims=True)
    return a * (1.0 / jnp.sqrt(diagonal))


def reduce_body(at, finish, omega_ref, out_ref, got, v, a_recv, S, turned, wsend, wrecv, own, own_row, plane_recv, w_all, psend, pall, small, small_plane, small_column, omega, omega_sem, sends, recvs, p_recv):
    X, Y, Z, C = at.dims
    TL = got.shape[0]
    NS = X * Z * C
    cells = Y * X * 8 * 1024
    x, y, z, c = at.x, at.y, at.z, at.c
    mine, here = z * C + c, y * X + x

    def dot(a, b, dims):
        return lax.dot_general(a, b, (dims, ((), ())), precision=lax.Precision.HIGHEST, preferred_element_type=F32)

    pltpu.make_async_copy(omega_ref, omega, omega_sem).wait()
    column = lax.broadcasted_iota(jnp.int32, (X * Z * C * TL, NS), 1)
    sketch_row = lax.broadcasted_iota(jnp.int32, (X * Z * C * TL, NS), 0)
    omegas = [
        dot(omega[...], jnp.where(sketch_row == column * TL + t, 1.0, 0.0), ((1,), (0,))) for t in range(TL)
    ]
    base_row = 8 * HALO_TILES + 8 * x + z
    base = [v[base_row, pl.ds(4 * c + q, 1), :] for q in range(4)]
    sketched = jnp.zeros((16, 512), F32)
    for t in range(TL):
        everything = got.at[t]
        pltpu.make_async_copy(everything, everything, a_recv.at[t]).wait()
        snaps = [got[t, pl.ds(q, NS, stride=4), :] - base[q] for q in range(4)]
        for q in range(4):
            S[q, NS * t : NS * t + NS] = snaps[q]
            turned[t, 128 * q : 128 * q + 128] = snaps[q].T
        sketched = sketched + dot(omegas[t], jnp.concatenate(snaps, axis=1), ((1,), (0,)))
    mat = jnp.concatenate([S[q] for q in range(4)], axis=1)
    across = jnp.concatenate([turned[t] for t in range(TL)], axis=1)
    part = dot(sketched, across, ((1,), (0,))) * (1.0 / cells)
    for h in range(2):
        wsend[h] = part[:, 128 * h : 128 * h + 128]

    def remote(src, dst, k, to, recv=None):
        return pltpu.make_async_remote_copy(
            src, dst, sends.at[k], recvs.at[k] if recv is None else recv, device_id=to, device_id_type=MESH
        )

    def over_column(k, src, dst):
        for dz, dc in at.column:
            to = {"z": at.zs[dz], "c": at.cs[dc]}
            remote(src(to["z"] * C + to["c"]), dst, k, to).start()

    def over_plane(k, src, dst):
        for dy, dx in at.plane:
            remote(src, dst, k, {"y": at.ys[dy], "x": at.xs[dx]}).start()

    def arrived(k, like):
        settle(like, recvs.at[k])

    def sent(k, like):
        settle(like, sends.at[k])

    strips = wrecv.at[:, pl.ds(0, Z * C - 1), :]
    in_plane = plane_recv.at[pl.ds(0, X * Y - 1)]
    in_column = small_column.at[pl.ds(0, Z * C - 1)]
    across_z = pall.at[pl.ds(0, 4), :, pl.ds(0, Z - 1), :]

    over_column(0, lambda row: wsend.at[:, pl.ds(row, 1), :], wrecv.at[:, pl.ds(mine, 1), :])
    wrecv[:, pl.ds(mine, 1), :] = wsend[:, pl.ds(mine, 1), :]
    finish()
    arrived(0, strips)
    value = jnp.sum(wrecv[...], axis=1)
    own[...] = value
    over_plane(1, own, plane_recv.at[here])
    plane_recv[here] = value
    sent(0, strips)
    arrived(1, in_plane)
    value = jnp.sum(plane_recv[...], axis=0)
    for h in range(2):
        own_row[h, 0:1, :] = value[h : h + 1]
    over_column(2, lambda row: own_row.at[:, pl.ds(0, 1), :], w_all.at[:, pl.ds(mine, 1), :])
    for h in range(2):
        w_all[h, pl.ds(mine, 1), :] = value[h : h + 1]
    sent(1, in_plane)
    arrived(2, strips)
    weights = jnp.concatenate([w_all[0], w_all[1]], axis=1)
    proj = dot(weights, mat, ((1,), (0,)))

    row = lax.broadcasted_iota(jnp.int32, (16, 128), 0)
    lane = lax.broadcasted_iota(jnp.int32, (16, 128), 1)
    diagonal = lane // 16 == lax.rem(row, 8)
    wide = dot(proj, jnp.concatenate([proj] * 8, axis=0), ((1,), (1,))) * (1.0 / cells)
    wide = jnp.where(diagonal, wide, 0.0)
    value = jnp.concatenate([jnp.sum(wide[8 * h : 8 * h + 8], axis=0, keepdims=True) for h in range(2)], axis=0)
    small[0] = value
    over_column(3, lambda row: small.at[0], small_column.at[mine])
    small_column[mine] = value

    for q in range(4):
        psend[q] = proj[:, 128 * q : 128 * q + 128]

    def strip(core, dz):
        return pall.at[pl.ds(4 * core, 4), :, at.zs[dz], :]

    other = {"c": at.cs[1]}
    z_order = far_first(Z)[:-1]
    projected = [remote(psend, strip(c, 0), 4, {"z": at.zs[dz]}, p_recv.at[dz]) for dz in z_order]
    for copy in projected:
        copy.start()
    remote(psend, strip(c, 0), 5, other).start()
    own_p = pltpu.make_async_copy(psend, strip(c, 0), p_recv.at[0])
    own_p.start()
    sent(2, strips)
    arrived(3, in_column)
    value = jnp.sum(small_column[...], axis=0)
    small[1] = value
    over_plane(6, small.at[1], small_plane.at[here])
    small_plane[here] = value
    for copy, dz in reversed(list(zip(projected, z_order))):
        copy.wait_recv()
        back = (Z - dz) % Z
        remote(strip(c, back), strip(c, back), 5, other).start()
    sent(3, in_column)
    sent(4, across_z)
    arrived(6, in_plane)
    value = jnp.sum(small_plane[...], axis=0)
    gram = jnp.concatenate([jnp.broadcast_to(value[h : h + 1], (8, 128)) for h in range(2)], axis=0)
    gram = jnp.where(diagonal, gram, 0.0)
    for shift in (64, 32, 16):
        gram = gram + pltpu.roll(gram, shift, 1)
    inverse = inverse_factor(gram)

    own_p.wait()
    sent(6, in_plane)
    sent(5, pall.at[pl.ds(0, 4)])
    arrived(5, pall.at[pl.ds(0, 4)])
    for i in range(16):
        total = inverse[i : i + 1, 16:17] * pall[:, 0]
        for m in range(1, i + 1):
            total = total + inverse[i : i + 1, 16 + m : 17 + m] * pall[:, m]
        out_ref[i] = total


def whole_body(dims, base_ref, pert_ref, omega_ref, out_ref, got, *scratch):
    one, two = scratch[:15], scratch[15:]
    at = Places(dims)
    pltpu.make_async_copy(omega_ref, scratch[-5], scratch[-4]).start()
    finish = snapshots_body(at, base_ref, pert_ref, got, *one)
    reduce_body(at, finish, omega_ref, out_ref, got, one[3], one[-1], *two)


def basis_of(base, pert, omega, dims):
    X, Y, Z, C = dims
    TL = pert.shape[0] // X
    NS, NZC, NXY = X * Z * C, Z * C, X * Y
    rows = 8 * (X + 2 * HALO_TILES)
    sem = pltpu.SemaphoreType.DMA
    anywhere = pl.BlockSpec(memory_space=pl.ANY)
    inside = pl.BlockSpec(memory_space=pltpu.VMEM)
    vmem = lambda *shape: pltpu.VMEM(shape, F32)
    return pl.pallas_call(
        functools.partial(whole_body, dims),
        out_shape=pltpu.VMEM((16, 8, 8, 128), F32),
        in_specs=[anywhere] * 3,
        out_specs=inside,
        scratch_shapes=[
            vmem(TL, NS * 4, 128),
            vmem(X * TL, 64, 128),
            vmem(64, 128),
            vmem(TL + 1, rows // 8, 64, 128),
            vmem(rows, 8, 128),
            vmem(rows, 8, 128),
            vmem(rows, 8, 128),
            vmem(TL, X, Z, 8, 128),
            sem((2,)),
            pltpu.SemaphoreType.REGULAR((max(Z, Y) // 2,)),
            sem,
            sem((TL + 1,)),
            sem((2,)),
            sem((TL + 1, 2)),
            sem,
            sem((TL,)),
            vmem(4, NS * TL, 128),
            vmem(TL, 512, NS),
            vmem(2, 16, 128),
            vmem(2, 16, 128),
            vmem(2, 128),
            vmem(2, 8, 128),
            vmem(NXY, 2, 128),
            vmem(2, 16, 128),
            vmem(4, 16, 128),
            vmem(8, 16, 8, 128),
            vmem(2, 2, 128),
            vmem(NXY, 2, 128),
            vmem(NZC, 2, 128),
            vmem(16, NS * TL),
            sem,
            sem((7,)),
            sem((7,)),
            sem((Z,)),
        ],
        compiler_params=pltpu.CompilerParams(collective_id=0, has_side_effects=True),
    )(base, pert, omega)


def tiles_first(a):
    lead = a.shape[:-2]
    a = a.reshape(*lead, 8, 8, 128)
    n = len(lead)
    return a.transpose(*range(n), n + 1, n, n + 2).reshape(*lead, 64, 128)


def body(dims, base_state, perturbations, sketch):
    out = basis_of(tiles_first(base_state), tiles_first(perturbations[0]), sketch.T, dims)
    return out.transpose(0, 2, 1, 3).reshape(16, 8, 1024)


def solution(mesh, along_x=ALONG_X):
    traj, space = mesh.shape["traj"], mesh.shape["space"]
    dims = (along_x, space // along_x, traj // CORES, CORES)
    X, Y, Z, C = dims
    torus = Mesh(mesh.devices.reshape(Z, C, Y, X), ("z", "c", "y", "x"))
    return jax.shard_map(
        functools.partial(body, dims),
        mesh=torus,
        in_specs=(P(("y", "x"), None), P(("z", "c"), None, ("y", "x"), None), P()),
        out_specs=P(None, ("y", "x"), None),
        check_vma=False,
    )
```

```python
import functools

import jax
import jax.numpy as jnp
from jax import lax
from jax.experimental import pallas as pl
from jax.experimental.pallas import tpu as pltpu
from jax.sharding import Mesh
from jax.sharding import PartitionSpec as P

STEPS = 4
CORES = 2
ALONG_X = 4
HALO_TILES = 2
MESH = pl.DeviceIdType.MESH
F32 = jnp.float32


def shifted(c):
    lane = lax.broadcasted_iota(jnp.int32, c.shape, c.ndim - 1)
    a, s = c.ndim - 1, c.ndim - 2
    e = pltpu.roll(c, 127, a)
    e = jnp.where(lane == 127, pltpu.roll(e, 7, s), e)
    w = pltpu.roll(c, 1, a)
    w = jnp.where(lane == 0, pltpu.roll(w, 1, s), w)
    return e, w


def parts_of(lo, hi, first, last):
    cuts = [lo]
    while cuts[-1] < hi:
        at = cuts[-1]
        if at < first:
            at = min(first, hi)
        elif at < last:
            at = min(at + 8, last)
        else:
            at = hi
        cuts.append(at)
    return list(zip(cuts[:-1], cuts[1:]))


def stage(src, field, dst, lo, hi, first, last, low, high, mix):
    keep, take = mix
    for r0, r1 in parts_of(lo, hi, first, last):
        c = src[r0:r1]
        e, w = shifted(c)
        p = e + src[r0 + 1 : r1 + 1]
        m = w + src[r0 - 1 : r1 - 1]
        out = (0.2 * take) * ((p + m) + c) - ((0.125 * take) * c) * (p - m)
        if keep:
            out = keep * field[r0:r1] + out
        if r1 <= first:
            out = out * low
        elif r0 >= last:
            out = out * high
        dst[r0:r1] = out


def advance(v, w1, w2, first, last, low, high):
    lo, hi = first - 3 * STEPS, last + 3 * STEPS
    for _ in range(STEPS):
        args = (first, last, low, high)
        stage(v, v, w1, lo + 1, hi - 1, *args, (0.0, 1.0))
        stage(w1, v, w2, lo + 2, hi - 2, *args, (0.75, 0.25))
        stage(w2, v, v, lo + 3, hi - 3, *args, (1.0 / 3.0, 2.0 / 3.0))
        lo, hi = lo + 3, hi - 3


def wrapped(at, size):
    return [at] + [jnp.where(at + d < size, at + d, at + d - size) for d in range(1, size)]


def far_first(size):
    return sorted(range(size), key=lambda d: (-min(d, size - d), d))


def settle(like, sem):
    pltpu.make_async_copy(like, like, sem).wait()


class Places:
    def __init__(self, dims):
        X, Y, Z, C = self.dims = dims
        self.x, self.y, self.z, self.c = (lax.axis_index(n) for n in "xyzc")
        self.xs, self.ys = wrapped(self.x, X), wrapped(self.y, Y)
        self.zs, self.cs = wrapped(self.z, Z), wrapped(self.c, C)
        self.column = [(dz, dc) for dz in far_first(Z) for dc in range(C) if dz or dc]
        self.plane = sorted(
            ((dy, dx) for dy in range(Y) for dx in range(X) if dy or dx),
            key=lambda d: -min(d[0], Y - d[0]) - min(d[1], X - d[1]),
        )
        self.ring = [(dc, dx) for dx in far_first(X) for dc in range(C) if dc or dx]
        self.sheet = sorted(
            ((dz, dy) for dz in range(Z) for dy in range(Y) if dz or dy),
            key=lambda d: -min(d[0], Z - d[0]) - min(d[1], Y - d[1]),
        )
        self.all = sorted(
            ((dz, dc, dx) for dz in range(Z) for dc in range(C) for dx in range(X) if dz or dc or dx),
            key=lambda d: (-min(d[0], Z - d[0]), d[1], -min(d[2], X - d[2]), d[2], d[0]),
        )


def snapshots_body(at, base_ref, pert_ref, got, pertv, basev, raw, v, w1, w2, send, in_sem, hello, xs_send, xs_recv, y_send, y_recv, a_send, a_recv):
    X, Y, Z, C = at.dims
    TL = raw.shape[0] - 1
    NS = X * Z * C
    first, last = 8 * HALO_TILES, 8 * (HALO_TILES + X)
    x, y, z, c = at.x, at.y, at.z, at.c
    me = (z * C + c) * X + x
    below, above = y > 0, y < Y - 1
    low = jnp.where(below, 1.0, 0.0).astype(F32)
    high = jnp.where(above, 1.0, 0.0).astype(F32)
    order = far_first(X)[:-1]
    rounds = max(Z, Y) // 2

    def signal(sem, to):
        pl.semaphore_signal(sem, inc=1, device_id=to, device_id_type=MESH)

    barrier = pltpu.get_barrier_semaphore()
    for dx in range(X):
        for dc in range(C):
            if dx or dc:
                signal(barrier, {"x": at.xs[dx], "c": at.cs[dc]})
    around = [{"z": at.zs[1]}, {"z": at.zs[Z - 1]}, {"y": at.ys[1]}, {"y": at.ys[Y - 1]}]
    for to in around:
        signal(barrier, to)

    base_in = pltpu.make_async_copy(base_ref, basev, in_sem.at[0])
    pert_in = pltpu.make_async_copy(pert_ref, pertv, in_sem.at[1])
    base_in.start()
    pert_in.start()
    base_in.wait()
    pert_in.wait()
    for k in range(X * TL):
        pertv[k] = pertv[k] + basev[...]
    pl.semaphore_wait(barrier, X * C - 1 + 4)

    def greet(k):
        for to in around:
            signal(hello.at[k], to)

    def greeted(k):
        pl.semaphore_wait(hello.at[k], 4)

    def x_copy(t, d):
        to = at.xs[d]
        source = basev if isinstance(t, int) and t == TL else pertv.at[to * TL + t]
        return pltpu.make_async_remote_copy(
            source, raw.at[t, HALO_TILES + x], xs_send, xs_recv.at[t],
            device_id={"x": to}, device_id_type=MESH,
        )

    def give_x(t):
        for d in order:
            x_copy(t, d).start()

    give_x(0)
    greet(0)
    for t in range(TL):
        raw[t, HALO_TILES + x] = pertv[x * TL + t]
    raw[TL, HALO_TILES + x] = basev[...]

    def up(t):
        buf = raw.at[t]
        return pltpu.make_async_remote_copy(
            buf.at[pl.ds(X, 2)], buf.at[pl.ds(0, 2)], y_send.at[0], y_recv.at[t, 0],
            device_id={"y": y + 1}, device_id_type=MESH,
        )

    def down(t):
        buf = raw.at[t]
        return pltpu.make_async_remote_copy(
            buf.at[pl.ds(2, 2)], buf.at[pl.ds(X + 2, 2)], y_send.at[1], y_recv.at[t, 1],
            device_id={"y": y - 1}, device_id_type=MESH,
        )

    def arrive_x(t):
        settle(raw.at[t, pl.ds(0, X - 1)], xs_recv.at[t])

    def pass_on(t):
        @pl.when(above)
        def _():
            up(t).start()

        @pl.when(below)
        def _():
            down(t).start()

    def arrive_y(t):
        buf = raw.at[t]

        @pl.when(below)
        def _():
            up(t).wait_recv()

        @pl.when(above)
        def _():
            down(t).wait_recv()

        @pl.when(jnp.logical_not(below))
        def _():
            buf[0:2] = jnp.zeros((2, 64, 128), F32)

        @pl.when(jnp.logical_not(above))
        def _():
            buf[X + 2 : X + 4] = jnp.zeros((2, 64, 128), F32)

    def rows_of(buf, row):
        return buf[row // 8, pl.ds(row % 8, 8, stride=8), :]

    for k in range(rounds - 2):
        greeted(k)
        greet(k + 1)
        if k + 1 < TL - 1:
            give_x(k + 1)
    for t in range(rounds - 1, TL - 1):
        give_x(t)
    arrive_x(0)
    pass_on(0)
    give_x(TL - 1)
    greeted(rounds - 2)
    greet(rounds - 1)
    arrive_x(1)
    pass_on(1)
    give_x(TL)

    def spot(t):
        return got.at[t, pl.ds(pl.multiple_of(4 * me, 4), 4), :]

    def cells(t, xx, zz, cc):
        return send.at[t, xx, zz, pl.ds(pl.multiple_of(4 * cc, 4), 4), :]

    def one(t, carry):
        arrive_y(t)

        @pl.when(t + 2 < TL + 1)
        def _():
            arrive_x(t + 2)
            pass_on(t + 2)

        for row in range(first - 12, last + 12):
            v[row] = rows_of(raw.at[t], row)
        advance(v, w1, w2, first, last, low, high)

        @pl.when(t == 0)
        def _():
            greeted(rounds - 1)

        @pl.when(t < TL)
        def _():
            for i in range(X):
                send[t, i] = v[first + 8 * i : first + 8 * i + 8]
            pltpu.make_async_copy(cells(t, x, z, c), spot(t), a_recv.at[t]).start()
            for dz, dc, dx in at.all:
                zz, cc, xx = at.zs[dz], at.cs[dc], at.xs[dx]
                pltpu.make_async_remote_copy(
                    cells(t, xx, zz, cc), spot(t), a_send, a_recv.at[t],
                    device_id={"x": xx, "z": zz, "c": cc}, device_id_type=MESH,
                ).start()

        return carry

    lax.fori_loop(0, TL + 1, one, 0)

    def finish():
        settle(raw.at[:, pl.ds(0, X - 1)], xs_send)

        @pl.when(above)
        def _():
            settle(raw.at[:, pl.ds(0, 2)], y_send.at[0])

        @pl.when(below)
        def _():
            settle(raw.at[:, pl.ds(0, 2)], y_send.at[1])

        settle(got.at[:, pl.ds(0, 4 * NS - 4)], a_send)

    return finish


def inverse_factor(gram):
    row = lax.broadcasted_iota(jnp.int32, (16, 128), 0)
    lane = lax.broadcasted_iota(jnp.int32, (16, 128), 1)
    a = jnp.where(lane < 16, gram, jnp.where(lane == row + 16, 1.0, 0.0))
    def wide(col):
        return jnp.broadcast_to(col, (16, 128))

    for k in range(0, 14, 2):
        p0, p1 = wide(a[k : k + 1, :]), wide(a[k + 1 : k + 2, :])
        f0, f1 = wide(a[:, k : k + 1]), wide(a[:, k + 1 : k + 2])
        u, v, w = wide(p0[:, k : k + 1]), wide(p0[:, k + 1 : k + 2]), wide(p1[:, k + 1 : k + 2])
        scale = 1.0 / (u * w - v * v)
        change = ((f0 * w - f1 * v) * scale) * p0 + ((f1 * u - f0 * v) * scale) * p1
        a = jnp.where(row > k + 1, a - change, a)
    before = pltpu.roll(a, 1, 0)
    cross = jnp.sum(jnp.where(lane == row - 1, a, 0.0), axis=1, keepdims=True)
    first = jnp.sum(jnp.where(lane == row - 1, before, 0.0), axis=1, keepdims=True)
    odd = lax.rem(row, 2) == 1
    a = jnp.where(odd, a - cross / first * before, a)
    diagonal = jnp.sum(jnp.where(lane == row, a, 0.0), axis=1, keepdims=True)
    return a * (1.0 / jnp.sqrt(diagonal))


def reduce_body(at, finish, omega_ref, out_ref, got, v, a_recv, S, turned, wsend, wrecv, own, own_row, sheet_recv, w_all, psend, pall, small, small_plane, small_column, omega, omega_sem, sends, recvs, p_recv):
    X, Y, Z, C = at.dims
    TL = got.shape[0]
    NS = X * Z * C
    cells = Y * X * 8 * 1024
    x, y, z, c = at.x, at.y, at.z, at.c
    mine, here = z * C + c, y * X + x

    def dot(a, b, dims):
        return lax.dot_general(a, b, (dims, ((), ())), precision=lax.Precision.HIGHEST, preferred_element_type=F32)

    pltpu.make_async_copy(omega_ref, omega, omega_sem).wait()
    column = lax.broadcasted_iota(jnp.int32, (X * Z * C * TL, NS), 1)
    sketch_row = lax.broadcasted_iota(jnp.int32, (X * Z * C * TL, NS), 0)
    omegas = [
        dot(omega[...], jnp.where(sketch_row == column * TL + t, 1.0, 0.0), ((1,), (0,))) for t in range(TL)
    ]
    base_row = 8 * HALO_TILES + 8 * x + z
    base = [v[base_row, pl.ds(4 * c + q, 1), :] for q in range(4)]
    sketched = jnp.zeros((16, 512), F32)
    for t in range(TL):
        everything = got.at[t]
        pltpu.make_async_copy(everything, everything, a_recv.at[t]).wait()
        snaps = [got[t, pl.ds(q, NS, stride=4), :] - base[q] for q in range(4)]
        for q in range(4):
            S[q, NS * t : NS * t + NS] = snaps[q]
            turned[t, 128 * q : 128 * q + 128] = snaps[q].T
        sketched = sketched + dot(omegas[t], jnp.concatenate(snaps, axis=1), ((1,), (0,)))
    mat = jnp.concatenate([S[q] for q in range(4)], axis=1)
    across = jnp.concatenate([turned[t] for t in range(TL)], axis=1)
    part = dot(sketched, across, ((1,), (0,))) * (1.0 / cells)
    for h in range(2):
        wsend[h] = part[:, 128 * h : 128 * h + 128]

    def remote(src, dst, k, to, recv=None):
        return pltpu.make_async_remote_copy(
            src, dst, sends.at[k], recvs.at[k] if recv is None else recv, device_id=to, device_id_type=MESH
        )

    def over_column(k, src, dst):
        for dz, dc in at.column:
            to = {"z": at.zs[dz], "c": at.cs[dc]}
            remote(src(to["z"] * C + to["c"]), dst, k, to).start()

    def over_plane(k, src, dst):
        for dy, dx in at.plane:
            remote(src, dst, k, {"y": at.ys[dy], "x": at.xs[dx]}).start()

    def arrived(k, like):
        settle(like, recvs.at[k])

    def sent(k, like):
        settle(like, sends.at[k])

    in_ring = wrecv.at[pl.ds(0, X * C - 1)]
    in_sheet = sheet_recv.at[pl.ds(0, Z * Y - 1)]
    in_plane = small_plane.at[pl.ds(0, X * Y - 1)]
    in_column = small_column.at[pl.ds(0, Z * C - 1)]
    across_z = pall.at[pl.ds(0, 4), :, pl.ds(0, Z - 1), :]

    share = 16 // (X * C)
    part_of = c * X + x
    for dc, dx in at.ring:
        to = {"c": at.cs[dc], "x": at.xs[dx]}
        theirs = pl.ds(share * (to["c"] * X + to["x"]), share)
        remote(wsend.at[:, theirs, :], wrecv.at[part_of], 0, to).start()
    wrecv[part_of] = wsend[:, pl.ds(share * part_of, share), :]
    finish()
    arrived(0, in_ring)
    value = jnp.sum(wrecv[...], axis=0)
    own[...] = value
    for dz, dy in at.sheet:
        remote(own, sheet_recv.at[z * Y + y], 1, {"z": at.zs[dz], "y": at.ys[dy]}).start()
    sheet_recv[z * Y + y] = value
    sent(0, in_ring)
    arrived(1, in_sheet)
    value = jnp.sum(sheet_recv[...], axis=0)
    for h in range(2):
        own_row[h, 0:share, :] = value[h]
    mine_rows = pl.ds(share * part_of, share)
    for dc, dx in at.ring:
        to = {"c": at.cs[dc], "x": at.xs[dx]}
        remote(own_row.at[:, pl.ds(0, share), :], w_all.at[:, mine_rows, :], 2, to).start()
    for h in range(2):
        w_all[h, mine_rows, :] = value[h]
    sent(1, in_sheet)
    arrived(2, in_ring)
    weights = jnp.concatenate([w_all[0], w_all[1]], axis=1)
    proj = dot(weights, mat, ((1,), (0,)))

    row = lax.broadcasted_iota(jnp.int32, (16, 128), 0)
    lane = lax.broadcasted_iota(jnp.int32, (16, 128), 1)
    diagonal = lane // 16 == lax.rem(row, 8)
    wide = dot(proj, jnp.concatenate([proj] * 8, axis=0), ((1,), (1,))) * (1.0 / cells)
    wide = jnp.where(diagonal, wide, 0.0)
    value = jnp.concatenate([jnp.sum(wide[8 * h : 8 * h + 8], axis=0, keepdims=True) for h in range(2)], axis=0)
    small[0] = value
    over_column(3, lambda row: small.at[0], small_column.at[mine])
    small_column[mine] = value

    for q in range(4):
        psend[q] = proj[:, 128 * q : 128 * q + 128]

    def strip(core, dz):
        return pall.at[pl.ds(4 * core, 4), :, at.zs[dz], :]

    other = {"c": at.cs[1]}
    z_order = far_first(Z)[:-1]
    projected = [remote(psend, strip(c, 0), 4, {"z": at.zs[dz]}, p_recv.at[dz]) for dz in z_order]
    sent(2, in_ring)
    sent(3, in_column)
    for copy in projected:
        copy.start()
    remote(psend, strip(c, 0), 5, other).start()
    own_p = pltpu.make_async_copy(psend, strip(c, 0), p_recv.at[0])
    own_p.start()
    arrived(3, in_column)
    value = jnp.sum(small_column[...], axis=0)
    small[1] = value
    over_plane(6, small.at[1], small_plane.at[here])
    small_plane[here] = value
    for copy, dz in reversed(list(zip(projected, z_order))):
        copy.wait_recv()
        back = (Z - dz) % Z
        remote(strip(c, back), strip(c, back), 5, other).start()
    sent(4, across_z)
    arrived(6, in_plane)
    value = jnp.sum(small_plane[...], axis=0)
    gram = jnp.concatenate([jnp.broadcast_to(value[h : h + 1], (8, 128)) for h in range(2)], axis=0)
    gram = jnp.where(diagonal, gram, 0.0)
    for shift in (64, 32, 16):
        gram = gram + pltpu.roll(gram, shift, 1)
    inverse = inverse_factor(gram)

    own_p.wait()
    sent(6, in_plane)
    sent(5, pall.at[pl.ds(0, 4)])
    arrived(5, pall.at[pl.ds(0, 4)])
    for i in range(16):
        total = inverse[i : i + 1, 16:17] * pall[:, 0]
        for m in range(1, i + 1):
            total = total + inverse[i : i + 1, 16 + m : 17 + m] * pall[:, m]
        out_ref[i] = total


def whole_body(dims, base_ref, pert_ref, omega_ref, out_ref, got, *scratch):
    one, two = scratch[:15], scratch[15:]
    at = Places(dims)
    pltpu.make_async_copy(omega_ref, scratch[-5], scratch[-4]).start()
    finish = snapshots_body(at, base_ref, pert_ref, got, *one)
    reduce_body(at, finish, omega_ref, out_ref, got, one[3], one[-1], *two)


def basis_of(base, pert, omega, dims):
    X, Y, Z, C = dims
    TL = pert.shape[0] // X
    NS, NZC, NXY = X * Z * C, Z * C, X * Y
    rows = 8 * (X + 2 * HALO_TILES)
    sem = pltpu.SemaphoreType.DMA
    anywhere = pl.BlockSpec(memory_space=pl.ANY)
    inside = pl.BlockSpec(memory_space=pltpu.VMEM)
    vmem = lambda *shape: pltpu.VMEM(shape, F32)
    return pl.pallas_call(
        functools.partial(whole_body, dims),
        out_shape=pltpu.VMEM((16, 8, 8, 128), F32),
        in_specs=[anywhere] * 3,
        out_specs=inside,
        scratch_shapes=[
            vmem(TL, NS * 4, 128),
            vmem(X * TL, 64, 128),
            vmem(64, 128),
            vmem(TL + 1, rows // 8, 64, 128),
            vmem(rows, 8, 128),
            vmem(rows, 8, 128),
            vmem(rows, 8, 128),
            vmem(TL, X, Z, 8, 128),
            sem((2,)),
            pltpu.SemaphoreType.REGULAR((max(Z, Y) // 2,)),
            sem,
            sem((TL + 1,)),
            sem((2,)),
            sem((TL + 1, 2)),
            sem,
            sem((TL,)),
            vmem(4, NS * TL, 128),
            vmem(TL, 512, NS),
            vmem(2, 16, 128),
            vmem(X * C, 2, 16 // (X * C), 128),
            vmem(2, 16 // (X * C), 128),
            vmem(2, 8, 128),
            vmem(Z * Y, 2, 16 // (X * C), 128),
            vmem(2, 16, 128),
            vmem(4, 16, 128),
            vmem(8, 16, 8, 128),
            vmem(2, 2, 128),
            vmem(NXY, 2, 128),
            vmem(NZC, 2, 128),
            vmem(16, NS * TL),
            sem,
            sem((7,)),
            sem((7,)),
            sem((Z,)),
        ],
        compiler_params=pltpu.CompilerParams(collective_id=0, has_side_effects=True),
    )(base, pert, omega)


def tiles_first(a):
    lead = a.shape[:-2]
    a = a.reshape(*lead, 8, 8, 128)
    n = len(lead)
    return a.transpose(*range(n), n + 1, n, n + 2).reshape(*lead, 64, 128)


def body(dims, base_state, perturbations, sketch):
    out = basis_of(tiles_first(base_state), tiles_first(perturbations[0]), sketch.T, dims)
    return out.transpose(0, 2, 1, 3).reshape(16, 8, 1024)


def solution(mesh, along_x=ALONG_X):
    traj, space = mesh.shape["traj"], mesh.shape["space"]
    dims = (along_x, space // along_x, traj // CORES, CORES)
    X, Y, Z, C = dims
    torus = Mesh(mesh.devices.reshape(Z, C, Y, X), ("z", "c", "y", "x"))
    return jax.shard_map(
        functools.partial(body, dims),
        mesh=torus,
        in_specs=(P(("y", "x"), None), P(("z", "c"), None, ("y", "x"), None), P()),
        out_specs=P(None, ("y", "x"), None),
        check_vma=False,
    )
```

```python
import functools

import jax
import jax.numpy as jnp
from jax import lax
from jax.experimental import pallas as pl
from jax.experimental.pallas import tpu as pltpu
from jax.sharding import Mesh
from jax.sharding import PartitionSpec as P

STEPS = 4
CORES = 2
ALONG_X = 4
HALO_TILES = 2
MESH = pl.DeviceIdType.MESH
F32 = jnp.float32


def shifted(c):
    lane = lax.broadcasted_iota(jnp.int32, c.shape, c.ndim - 1)
    a, s = c.ndim - 1, c.ndim - 2
    e = pltpu.roll(c, 127, a)
    e = jnp.where(lane == 127, pltpu.roll(e, 7, s), e)
    w = pltpu.roll(c, 1, a)
    w = jnp.where(lane == 0, pltpu.roll(w, 1, s), w)
    return e, w


def parts_of(lo, hi, first, last):
    cuts = [lo]
    while cuts[-1] < hi:
        at = cuts[-1]
        if at < first:
            at = min(first, hi)
        elif at < last:
            at = min(at + 4, last)
        else:
            at = hi
        cuts.append(at)
    return list(zip(cuts[:-1], cuts[1:]))


def stage(src, field, dst, lo, hi, first, last, low, high, mix):
    keep, take = mix
    for r0, r1 in parts_of(lo, hi, first, last):
        c = src[r0:r1]
        e, w = shifted(c)
        p = e + src[r0 + 1 : r1 + 1]
        m = w + src[r0 - 1 : r1 - 1]
        out = (0.2 * take) * ((p + m) + c) - ((0.125 * take) * c) * (p - m)
        if keep:
            out = keep * field[r0:r1] + out
        if r1 <= first:
            out = out * low
        elif r0 >= last:
            out = out * high
        dst[r0:r1] = out


def advance(v, w1, w2, first, last, low, high):
    lo, hi = first - 3 * STEPS, last + 3 * STEPS
    for _ in range(STEPS):
        args = (first, last, low, high)
        stage(v, v, w1, lo + 1, hi - 1, *args, (0.0, 1.0))
        stage(w1, v, w2, lo + 2, hi - 2, *args, (0.75, 0.25))
        stage(w2, v, v, lo + 3, hi - 3, *args, (1.0 / 3.0, 2.0 / 3.0))
        lo, hi = lo + 3, hi - 3


def wrapped(at, size):
    return [at] + [jnp.where(at + d < size, at + d, at + d - size) for d in range(1, size)]


def far_first(size):
    return sorted(range(size), key=lambda d: (-min(d, size - d), d))


def settle(like, sem):
    pltpu.make_async_copy(like, like, sem).wait()


class Places:
    def __init__(self, dims):
        X, Y, Z, C = self.dims = dims
        self.x, self.y, self.z, self.c = (lax.axis_index(n) for n in "xyzc")
        self.xs, self.ys = wrapped(self.x, X), wrapped(self.y, Y)
        self.zs, self.cs = wrapped(self.z, Z), wrapped(self.c, C)
        self.column = [(dz, dc) for dz in far_first(Z) for dc in range(C) if dz or dc]
        self.plane = sorted(
            ((dy, dx) for dy in range(Y) for dx in range(X) if dy or dx),
            key=lambda d: -min(d[0], Y - d[0]) - min(d[1], X - d[1]),
        )
        self.ring = [(dc, dx) for dx in far_first(X) for dc in range(C) if dc or dx]
        self.sheet = sorted(
            ((dz, dy) for dz in range(Z) for dy in range(Y) if dz or dy),
            key=lambda d: -min(d[0], Z - d[0]) - min(d[1], Y - d[1]),
        )
        self.all = sorted(
            ((dz, dc, dx) for dz in range(Z) for dc in range(C) for dx in range(X) if dz or dc or dx),
            key=lambda d: (-min(d[0], Z - d[0]), d[1], -min(d[2], X - d[2]), d[2], d[0]),
        )


def snapshots_body(at, base_ref, pert_ref, got, pertv, basev, raw, v, w1, w2, send, in_sem, hello, xs_send, xs_recv, y_send, y_recv, a_send, a_recv):
    X, Y, Z, C = at.dims
    TL = raw.shape[0] - 1
    NS = X * Z * C
    first, last = 8 * HALO_TILES, 8 * (HALO_TILES + X)
    x, y, z, c = at.x, at.y, at.z, at.c
    me = (z * C + c) * X + x
    below, above = y > 0, y < Y - 1
    low = jnp.where(below, 1.0, 0.0).astype(F32)
    high = jnp.where(above, 1.0, 0.0).astype(F32)
    order = far_first(X)[:-1]
    rounds = max(Z, Y) // 2

    def signal(sem, to):
        pl.semaphore_signal(sem, inc=1, device_id=to, device_id_type=MESH)

    barrier = pltpu.get_barrier_semaphore()
    for dx in range(X):
        for dc in range(C):
            if dx or dc:
                signal(barrier, {"x": at.xs[dx], "c": at.cs[dc]})
    around = [{"z": at.zs[1]}, {"z": at.zs[Z - 1]}, {"y": at.ys[1]}, {"y": at.ys[Y - 1]}]
    for to in around:
        signal(barrier, to)

    base_in = pltpu.make_async_copy(base_ref, basev, in_sem.at[0])
    pert_in = pltpu.make_async_copy(pert_ref, pertv, in_sem.at[1])
    base_in.start()
    pert_in.start()
    base_in.wait()
    pert_in.wait()
    for k in range(X * TL):
        pertv[k] = pertv[k] + basev[...]
    pl.semaphore_wait(barrier, X * C - 1 + 4)

    def greet(k):
        for to in around:
            signal(hello.at[k], to)

    def greeted(k):
        pl.semaphore_wait(hello.at[k], 4)

    def x_copy(t, d):
        to = at.xs[d]
        source = basev if isinstance(t, int) and t == TL else pertv.at[to * TL + t]
        return pltpu.make_async_remote_copy(
            source, raw.at[t, HALO_TILES + x], xs_send, xs_recv.at[t],
            device_id={"x": to}, device_id_type=MESH,
        )

    def give_x(t):
        for d in order:
            x_copy(t, d).start()

    give_x(0)
    greet(0)
    for t in range(TL):
        raw[t, HALO_TILES + x] = pertv[x * TL + t]
    raw[TL, HALO_TILES + x] = basev[...]

    def up(t):
        buf = raw.at[t]
        return pltpu.make_async_remote_copy(
            buf.at[pl.ds(X, 2)], buf.at[pl.ds(0, 2)], y_send.at[0], y_recv.at[t, 0],
            device_id={"y": y + 1}, device_id_type=MESH,
        )

    def down(t):
        buf = raw.at[t]
        return pltpu.make_async_remote_copy(
            buf.at[pl.ds(2, 2)], buf.at[pl.ds(X + 2, 2)], y_send.at[1], y_recv.at[t, 1],
            device_id={"y": y - 1}, device_id_type=MESH,
        )

    def arrive_x(t):
        settle(raw.at[t, pl.ds(0, X - 1)], xs_recv.at[t])

    def pass_on(t):
        @pl.when(above)
        def _():
            up(t).start()

        @pl.when(below)
        def _():
            down(t).start()

    def arrive_y(t):
        buf = raw.at[t]

        @pl.when(below)
        def _():
            up(t).wait_recv()

        @pl.when(above)
        def _():
            down(t).wait_recv()

        @pl.when(jnp.logical_not(below))
        def _():
            buf[0:2] = jnp.zeros((2, 64, 128), F32)

        @pl.when(jnp.logical_not(above))
        def _():
            buf[X + 2 : X + 4] = jnp.zeros((2, 64, 128), F32)

    def rows_of(buf, row):
        return buf[row // 8, pl.ds(row % 8, 8, stride=8), :]

    for k in range(rounds - 2):
        greeted(k)
        greet(k + 1)
        if k + 1 < TL - 1:
            give_x(k + 1)
    for t in range(rounds - 1, TL - 1):
        give_x(t)
    arrive_x(0)
    pass_on(0)
    give_x(TL - 1)
    greeted(rounds - 2)
    greet(rounds - 1)
    arrive_x(1)
    pass_on(1)
    give_x(TL)

    def spot(t):
        return got.at[t, pl.ds(pl.multiple_of(4 * me, 4), 4), :]

    def cells(t, xx, zz, cc):
        return send.at[t, xx, zz, pl.ds(pl.multiple_of(4 * cc, 4), 4), :]

    def one(t, carry):
        @pl.when(t + 2 < TL + 1)
        def _():
            arrive_x(t + 2)
            pass_on(t + 2)

        arrive_y(t)
        for row in range(first - 12, last + 12):
            v[row] = rows_of(raw.at[t], row)
        advance(v, w1, w2, first, last, low, high)

        @pl.when(t == 0)
        def _():
            greeted(rounds - 1)

        @pl.when(t < TL)
        def _():
            for i in range(X):
                send[t, i] = v[first + 8 * i : first + 8 * i + 8]
            pltpu.make_async_copy(cells(t, x, z, c), spot(t), a_recv.at[t]).start()
            for dz, dc, dx in at.all:
                zz, cc, xx = at.zs[dz], at.cs[dc], at.xs[dx]
                pltpu.make_async_remote_copy(
                    cells(t, xx, zz, cc), spot(t), a_send, a_recv.at[t],
                    device_id={"x": xx, "z": zz, "c": cc}, device_id_type=MESH,
                ).start()

        return carry

    lax.fori_loop(0, TL + 1, one, 0)

    def finish():
        settle(raw.at[:, pl.ds(0, X - 1)], xs_send)

        @pl.when(above)
        def _():
            settle(raw.at[:, pl.ds(0, 2)], y_send.at[0])

        @pl.when(below)
        def _():
            settle(raw.at[:, pl.ds(0, 2)], y_send.at[1])

        settle(got.at[:, pl.ds(0, 4 * NS - 4)], a_send)

    return finish


def inverse_factor(gram):
    row = lax.broadcasted_iota(jnp.int32, (16, 128), 0)
    lane = lax.broadcasted_iota(jnp.int32, (16, 128), 1)
    a = jnp.where(lane < 16, gram, jnp.where(lane == row + 16, 1.0, 0.0))
    def wide(col):
        return jnp.broadcast_to(col, (16, 128))

    for k in range(0, 14, 2):
        p0, p1 = wide(a[k : k + 1, :]), wide(a[k + 1 : k + 2, :])
        f0, f1 = wide(a[:, k : k + 1]), wide(a[:, k + 1 : k + 2])
        u, v, w = wide(p0[:, k : k + 1]), wide(p0[:, k + 1 : k + 2]), wide(p1[:, k + 1 : k + 2])
        scale = 1.0 / (u * w - v * v)
        change = ((f0 * w - f1 * v) * scale) * p0 + ((f1 * u - f0 * v) * scale) * p1
        a = jnp.where(row > k + 1, a - change, a)
    before = pltpu.roll(a, 1, 0)
    cross = jnp.sum(jnp.where(lane == row - 1, a, 0.0), axis=1, keepdims=True)
    first = jnp.sum(jnp.where(lane == row - 1, before, 0.0), axis=1, keepdims=True)
    odd = lax.rem(row, 2) == 1
    a = jnp.where(odd, a - cross / first * before, a)
    diagonal = jnp.sum(jnp.where(lane == row, a, 0.0), axis=1, keepdims=True)
    return a * (1.0 / jnp.sqrt(diagonal))


def reduce_body(at, finish, omega_ref, out_ref, got, v, a_recv, S, turned, wsend, wrecv, own, own_row, sheet_recv, w_all, psend, pall, small, small_plane, small_column, omega, omega_sem, sends, recvs, p_recv):
    X, Y, Z, C = at.dims
    TL = got.shape[0]
    NS = X * Z * C
    cells = Y * X * 8 * 1024
    x, y, z, c = at.x, at.y, at.z, at.c
    mine, here = z * C + c, y * X + x

    def dot(a, b, dims):
        return lax.dot_general(a, b, (dims, ((), ())), precision=lax.Precision.HIGHEST, preferred_element_type=F32)

    pltpu.make_async_copy(omega_ref, omega, omega_sem).wait()
    column = lax.broadcasted_iota(jnp.int32, (X * Z * C * TL, NS), 1)
    sketch_row = lax.broadcasted_iota(jnp.int32, (X * Z * C * TL, NS), 0)
    omegas = [
        dot(omega[...], jnp.where(sketch_row == column * TL + t, 1.0, 0.0), ((1,), (0,))) for t in range(TL)
    ]
    base_row = 8 * HALO_TILES + 8 * x + z
    base = [v[base_row, pl.ds(4 * c + q, 1), :] for q in range(4)]
    sketched = jnp.zeros((16, 512), F32)
    for t in range(TL):
        everything = got.at[t]
        pltpu.make_async_copy(everything, everything, a_recv.at[t]).wait()
        snaps = [got[t, pl.ds(q, NS, stride=4), :] - base[q] for q in range(4)]
        for q in range(4):
            S[q, NS * t : NS * t + NS] = snaps[q]
            turned[t, 128 * q : 128 * q + 128] = snaps[q].T
        sketched = sketched + dot(omegas[t], jnp.concatenate(snaps, axis=1), ((1,), (0,)))
    mat = jnp.concatenate([S[q] for q in range(4)], axis=1)
    across = jnp.concatenate([turned[t] for t in range(TL)], axis=1)
    part = dot(sketched, across, ((1,), (0,))) * (1.0 / cells)
    for h in range(2):
        wsend[h] = part[:, 128 * h : 128 * h + 128]

    def remote(src, dst, k, to, recv=None):
        return pltpu.make_async_remote_copy(
            src, dst, sends.at[k], recvs.at[k] if recv is None else recv, device_id=to, device_id_type=MESH
        )

    def over_column(k, src, dst):
        for dz, dc in at.column:
            to = {"z": at.zs[dz], "c": at.cs[dc]}
            remote(src(to["z"] * C + to["c"]), dst, k, to).start()

    def over_plane(k, src, dst):
        for dy, dx in at.plane:
            remote(src, dst, k, {"y": at.ys[dy], "x": at.xs[dx]}).start()

    def arrived(k, like):
        settle(like, recvs.at[k])

    def sent(k, like):
        settle(like, sends.at[k])

    in_ring = wrecv.at[pl.ds(0, X * C - 1)]
    in_sheet = sheet_recv.at[pl.ds(0, Z * Y - 1)]
    in_plane = small_plane.at[pl.ds(0, X * Y - 1)]
    in_column = small_column.at[pl.ds(0, Z * C - 1)]
    across_z = pall.at[pl.ds(0, 4), :, pl.ds(0, Z - 1), :]

    share = 16 // (X * C)
    part_of = c * X + x
    for dc, dx in at.ring:
        to = {"c": at.cs[dc], "x": at.xs[dx]}
        theirs = pl.ds(share * (to["c"] * X + to["x"]), share)
        remote(wsend.at[:, theirs, :], wrecv.at[part_of], 0, to).start()
    wrecv[part_of] = wsend[:, pl.ds(share * part_of, share), :]
    finish()
    arrived(0, in_ring)
    value = jnp.sum(wrecv[...], axis=0)
    own[...] = value
    for dz, dy in at.sheet:
        remote(own, sheet_recv.at[z * Y + y], 1, {"z": at.zs[dz], "y": at.ys[dy]}).start()
    sheet_recv[z * Y + y] = value
    sent(0, in_ring)
    arrived(1, in_sheet)
    value = jnp.sum(sheet_recv[...], axis=0)
    for h in range(2):
        own_row[h, 0:share, :] = value[h]
    mine_rows = pl.ds(share * part_of, share)
    for dc, dx in at.ring:
        to = {"c": at.cs[dc], "x": at.xs[dx]}
        remote(own_row.at[:, pl.ds(0, share), :], w_all.at[:, mine_rows, :], 2, to).start()
    for h in range(2):
        w_all[h, mine_rows, :] = value[h]
    sent(1, in_sheet)
    arrived(2, in_ring)
    weights = jnp.concatenate([w_all[0], w_all[1]], axis=1)
    proj = dot(weights, mat, ((1,), (0,)))

    row = lax.broadcasted_iota(jnp.int32, (16, 128), 0)
    lane = lax.broadcasted_iota(jnp.int32, (16, 128), 1)
    diagonal = lane // 16 == lax.rem(row, 8)
    wide = dot(proj, jnp.concatenate([proj] * 8, axis=0), ((1,), (1,))) * (1.0 / cells)
    wide = jnp.where(diagonal, wide, 0.0)
    value = jnp.concatenate([jnp.sum(wide[8 * h : 8 * h + 8], axis=0, keepdims=True) for h in range(2)], axis=0)
    small[0] = value
    over_column(3, lambda row: small.at[0], small_column.at[mine])
    small_column[mine] = value

    for q in range(4):
        psend[q] = proj[:, 128 * q : 128 * q + 128]

    def strip(core, dz):
        return pall.at[pl.ds(4 * core, 4), :, at.zs[dz], :]

    other = {"c": at.cs[1]}
    z_order = far_first(Z)[:-1]
    projected = [remote(psend, strip(c, 0), 4, {"z": at.zs[dz]}, p_recv.at[dz]) for dz in z_order]
    sent(2, in_ring)
    sent(3, in_column)
    for copy in projected:
        copy.start()
    remote(psend, strip(c, 0), 5, other).start()
    own_p = pltpu.make_async_copy(psend, strip(c, 0), p_recv.at[0])
    own_p.start()
    arrived(3, in_column)
    value = jnp.sum(small_column[...], axis=0)
    small[1] = value
    over_plane(6, small.at[1], small_plane.at[here])
    small_plane[here] = value
    for copy, dz in reversed(list(zip(projected, z_order))):
        copy.wait_recv()
        back = (Z - dz) % Z
        remote(strip(c, back), strip(c, back), 5, other).start()
    sent(4, across_z)
    arrived(6, in_plane)
    value = jnp.sum(small_plane[...], axis=0)
    gram = jnp.concatenate([jnp.broadcast_to(value[h : h + 1], (8, 128)) for h in range(2)], axis=0)
    gram = jnp.where(diagonal, gram, 0.0)
    for shift in (64, 32, 16):
        gram = gram + pltpu.roll(gram, shift, 1)
    inverse = inverse_factor(gram)

    own_p.wait()
    sent(6, in_plane)
    sent(5, pall.at[pl.ds(0, 4)])
    arrived(5, pall.at[pl.ds(0, 4)])
    for i in range(16):
        total = inverse[i : i + 1, 16:17] * pall[:, 0]
        for m in range(1, i + 1):
            total = total + inverse[i : i + 1, 16 + m : 17 + m] * pall[:, m]
        out_ref[i] = total


def whole_body(dims, base_ref, pert_ref, omega_ref, out_ref, got, *scratch):
    one, two = scratch[:15], scratch[15:]
    at = Places(dims)
    pltpu.make_async_copy(omega_ref, scratch[-5], scratch[-4]).start()
    finish = snapshots_body(at, base_ref, pert_ref, got, *one)
    reduce_body(at, finish, omega_ref, out_ref, got, one[3], one[-1], *two)


def basis_of(base, pert, omega, dims):
    X, Y, Z, C = dims
    TL = pert.shape[0] // X
    NS, NZC, NXY = X * Z * C, Z * C, X * Y
    rows = 8 * (X + 2 * HALO_TILES)
    sem = pltpu.SemaphoreType.DMA
    anywhere = pl.BlockSpec(memory_space=pl.ANY)
    inside = pl.BlockSpec(memory_space=pltpu.VMEM)
    vmem = lambda *shape: pltpu.VMEM(shape, F32)
    return pl.pallas_call(
        functools.partial(whole_body, dims),
        out_shape=pltpu.VMEM((16, 8, 8, 128), F32),
        in_specs=[anywhere] * 3,
        out_specs=inside,
        scratch_shapes=[
            vmem(TL, NS * 4, 128),
            vmem(X * TL, 64, 128),
            vmem(64, 128),
            vmem(TL + 1, rows // 8, 64, 128),
            vmem(rows, 8, 128),
            vmem(rows, 8, 128),
            vmem(rows, 8, 128),
            vmem(TL, X, Z, 8, 128),
            sem((2,)),
            pltpu.SemaphoreType.REGULAR((max(Z, Y) // 2,)),
            sem,
            sem((TL + 1,)),
            sem((2,)),
            sem((TL + 1, 2)),
            sem,
            sem((TL,)),
            vmem(4, NS * TL, 128),
            vmem(TL, 512, NS),
            vmem(2, 16, 128),
            vmem(X * C, 2, 16 // (X * C), 128),
            vmem(2, 16 // (X * C), 128),
            vmem(2, 8, 128),
            vmem(Z * Y, 2, 16 // (X * C), 128),
            vmem(2, 16, 128),
            vmem(4, 16, 128),
            vmem(8, 16, 8, 128),
            vmem(2, 2, 128),
            vmem(NXY, 2, 128),
            vmem(NZC, 2, 128),
            vmem(16, NS * TL),
            sem,
            sem((7,)),
            sem((7,)),
            sem((Z,)),
        ],
        compiler_params=pltpu.CompilerParams(collective_id=0, has_side_effects=True),
    )(base, pert, omega)


def tiles_first(a):
    lead = a.shape[:-2]
    a = a.reshape(*lead, 8, 8, 128)
    n = len(lead)
    return a.transpose(*range(n), n + 1, n, n + 2).reshape(*lead, 64, 128)


def body(dims, base_state, perturbations, sketch):
    out = basis_of(tiles_first(base_state), tiles_first(perturbations[0]), sketch.T, dims)
    return out.transpose(0, 2, 1, 3).reshape(16, 8, 1024)


def solution(mesh, along_x=ALONG_X):
    traj, space = mesh.shape["traj"], mesh.shape["space"]
    dims = (along_x, space // along_x, traj // CORES, CORES)
    X, Y, Z, C = dims
    torus = Mesh(mesh.devices.reshape(Z, C, Y, X), ("z", "c", "y", "x"))
    return jax.shard_map(
        functools.partial(body, dims),
        mesh=torus,
        in_specs=(P(("y", "x"), None), P(("z", "c"), None, ("y", "x"), None), P()),
        out_specs=P(None, ("y", "x"), None),
        check_vma=False,
    )
```
